256 devices in a mesh: elem: 64 (over z, y_lo, x), band: 4 (over y_hi, core).
Axes of the slice: x: 4, y: 4 (y_hi: 2, y_lo: 2; y = y_hi * 2 + y_lo), z: 8, core: 2. Of those that a mesh axis runs over, the one named last changes fastest.
Arguments:
- basis_counts: int32 [512, 16], P('elem', 'band'), may hold values from 1 to 128, as said below
- neighbour_codes: int32 [512, 16, 6], P('elem', 'band'), may hold values from 0 to 8, as said below
- x_block: bfloat16 [512, 16, 160, 128], P('elem', 'band'), may hold values from -6 to 6
- h_self: bfloat16 [512, 16, 128, 128], P('elem', 'band'), may hold values from -0.375 to 0.375
- h_near: bfloat16 [512, 16, 6, 128, 128], P('elem', 'band'), may hold values from -0.375 to 0.375
Outputs:
- filtered: bfloat16 [512, 16, 160, 128], P('elem', 'band')
- gram: float32 [160, 160], P('band')
- ritz: float32 [160, 160], P('band')
The draws below stay inside these ranges and needn't reach their ends.
Inputs may be any that keep to these rules, and one draw needn't show every extreme that they name: `basis_counts`: at least one element holds exactly 128 basis functions. `neighbour_codes`: an element's 6 codes are distinct and never 4; code q names the element offset by q // 3 - 1 along the first dimension and q % 3 - 1 along the second, periodically.
All inputs are finite; a program needn't handle non-finite values.
Results may differ from the reference program's by a relative error of at most 0.007.
Values may be sent and summed in bfloat16 or wider, within the bound.
No kernel may reach another device: no remote copies, remote signals or barrier semaphores. Data moves between devices by JAX's collectives and lax.ppermute only.
A program may use at most 128 MiB of HBM per device.

```python
import jax
import jax.numpy as jnp
from jax import lax

NB_MAX = 128
COLS = 160
K = 6
EX = 512
EY = 16
ELEMS = 8192


def draw_basis_counts(key, part):
    key_base, key_factor, key_pick = jax.random.split(key, 3)
    base = jax.random.randint(key_base, (EX, EY), 1, NB_MAX // 2 + 1)
    factor = jax.random.randint(key_factor, (EX, 1), 1, 4)
    counts = jnp.minimum(base * factor, NB_MAX).reshape(-1)
    pick = jax.random.randint(key_pick, (), 0, EX * EY)
    counts = counts.at[pick].set(NB_MAX)
    return counts.reshape(EX, EY).astype(jnp.int32)


def draw_neighbour_codes(key, part):
    scores = jax.random.randint(key, (EX, EY, 8), 0, 1 << 20) * 8 + jnp.arange(8, dtype=jnp.int32)
    order = jnp.argsort(scores, axis=-1)[:, :, :K]
    codes = order + (order >= 4).astype(jnp.int32)
    return codes.astype(jnp.int32)


def strengthened(array, own_key, source, target, parts, factor):
    owner, partner = [(jnp.arange(array.shape[position]) // (array.shape[position] // parts)).reshape([-1 if axis == position else 1 for axis in range(array.ndim)]) for position in (source, target)]
    chosen = jax.random.permutation(own_key, parts)[partner]
    strong = (owner == chosen) | (owner == (partner + parts // 2) % parts)
    return jnp.where(strong, factor * array, array)


def shard_levels(key, dims, shards, low, top_value):
    def one(axis_at, shards_of):
        steps = jax.random.uniform(jax.random.fold_in(jax.random.fold_in(key, 6), axis_at), (shards_of,), jnp.float32, low / len(shards), top_value / len(shards))
        return jnp.repeat(jnp.exp(steps), dims[axis_at] // shards_of).reshape((-1,) + (1,) * (len(dims) - axis_at - 1))

    level = one(*shards[0])
    for cut in shards[1:]:
        level = level * one(*cut)
    return level


def centred(own_key, dims, width, limit, pieces=(), kind=jnp.bfloat16):
    factor_of = shard_levels(own_key, dims, pieces, -0.22, 0.18) if pieces else 1.0
    array = jax.random.normal(own_key, dims, jnp.float32) * width * factor_of
    return jnp.minimum(jnp.maximum(array, -limit), limit).astype(kind)


def bell_draw_with(key, shape, scale, limit, shards, heavy, kind=jnp.bfloat16):
    drawn = scale * jax.random.normal(key, shape, jnp.float32)
    if shards:
        drawn = drawn * shard_levels(key, shape, shards, -0.22, 0.18)
    return jnp.clip(strengthened(drawn, jax.random.fold_in(key, 3), *heavy), -limit, limit).astype(kind)


def setup_inputs(seed: int = 0) -> dict:
    arg_keys = jax.random.split(jax.random.key(seed), 6)
    return {
        "basis_counts": draw_basis_counts(jax.random.fold_in(arg_keys[5], 71), 0),
        "neighbour_codes": draw_neighbour_codes(jax.random.fold_in(arg_keys[5], 71), 0),
        "x_block": bell_draw_with(arg_keys[2], (EX, EY, COLS, NB_MAX), 1.0, 6.0, ((0, 64), (1, 4)), (0, 2, 32, 2.75)),
        "h_self": centred(arg_keys[3], (EX, EY, NB_MAX, NB_MAX), ((K + 1) * NB_MAX // 3) ** -0.5, 0.375, ((0, 64), (1, 4))),
        "h_near": centred(arg_keys[4], (EX, EY, K, NB_MAX, NB_MAX), ((K + 1) * NB_MAX // 3) ** -0.5, 0.375, ((0, 64), (1, 4))),
    }


cheb_center = 0.25
cheb_half = 1.5


def operate(vector_block, h_self, h_near, neighbour_codes, live_mask):
    extended = jnp.pad(vector_block, ((1, 1), (1, 1), (0, 0), (0, 0)), mode="wrap")
    width_ext = EY + 2

    def one_row(packed):
        row_index, own_row, self_row, near_row, code_row, mask_row = packed
        window = lax.dynamic_slice_in_dim(extended, row_index, 3, 0).reshape(3 * width_ext, COLS, NB_MAX)
        gather_index = (code_row // 3) * width_ext + jnp.arange(EY, dtype=jnp.int32)[:, None] + code_row % 3
        nearby = jnp.take(window, gather_index.astype(jnp.int32), axis=0)
        summed = jnp.einsum("ecs,esr->ecr", own_row.astype(jnp.float32), self_row.astype(jnp.float32))
        summed = summed + jnp.einsum("ekcs,eksr->ecr", nearby.astype(jnp.float32), near_row.astype(jnp.float32))
        return jnp.where(mask_row, summed, jnp.float32(0.0))

    row_ids = jnp.arange(EX, dtype=jnp.int32)
    return lax.map(one_row, (row_ids, vector_block, h_self, h_near, neighbour_codes, live_mask))


def reference(basis_counts, neighbour_codes, x_block, h_self, h_near):
    live_mask = jnp.arange(NB_MAX, dtype=jnp.int32)[None, None, None, :] < basis_counts[:, :, None, None]
    start = jnp.where(live_mask, x_block, jnp.zeros_like(x_block))

    def apply_op(vector_block):
        return operate(vector_block, h_self, h_near, neighbour_codes, live_mask)

    first = ((apply_op(start) - cheb_center * start.astype(jnp.float32)) / cheb_half).astype(jnp.bfloat16)
    second = (2.0 * (apply_op(first) - cheb_center * first.astype(jnp.float32)) / cheb_half - start.astype(jnp.float32)).astype(jnp.bfloat16)
    filtered = (2.0 * (apply_op(second) - cheb_center * second.astype(jnp.float32)) / cheb_half - first.astype(jnp.float32)).astype(jnp.bfloat16)
    image = apply_op(filtered).astype(jnp.bfloat16)

    def accumulate(carry, packed):
        filt_row, image_row = packed
        left = filt_row.astype(jnp.float32)
        gram_part = jnp.einsum("ecr,edr->cd", left, left)
        ritz_part = jnp.einsum("ecr,edr->cd", left, image_row.astype(jnp.float32))
        return (carry[0] + gram_part, carry[1] + ritz_part), None

    zeros = jnp.zeros((COLS, COLS), jnp.float32)
    (gram_sum, ritz_sum), unused = lax.scan(accumulate, (zeros, zeros), (filtered, image))
    normalizer = jnp.float32(ELEMS * NB_MAX / 3.0)
    return filtered, gram_sum / normalizer, ritz_sum / normalizer
```

```python
import functools

import jax
import jax.numpy as jnp
from jax import lax
from jax.experimental import pallas as pl
from jax.experimental.pallas import tpu as pltpu
from jax.sharding import Mesh, PartitionSpec as P

CENTER = 0.25
INV_HALF = 1.0 / 1.5
ANY = pl.BlockSpec(memory_space=pl.ANY)


def nt_dot(a, b):
    return lax.dot_general(a, b, (((1,), (1,)), ((), ())), preferred_element_type=jnp.float32)


def step_kernel(mode, dims, index_ref, count_ref, band_ref, *refs):
    rows, cols, columns, basis, neighbours = dims
    wide = cols + 2
    refs = list(refs)
    x_hbm, low_hbm, high_hbm, left_hbm, right_hbm, corner_low, corner_high = refs[:7]
    self_ref, near_ref = refs[7:9]
    del refs[:9]
    prev_ref = refs.pop(0) if mode in ("second", "third") else None
    gram_in = refs.pop(0) if mode == "image" else None
    out_ref = refs.pop(0) if mode != "image" else None
    gram_ref = refs.pop(0) if mode == "third" else None
    pieces = [refs.pop(0) for _ in range(4)] if mode == "image" else None
    ext, sem = refs[:2]
    acc = refs[2] if mode == "image" else None
    i = pl.program_id(0)

    @pl.when(i == 0)
    def _():
        copies = []

        def move(src, slot, count):
            copies.append(pltpu.make_async_copy(src, ext.at[pl.ds(slot, count)], sem))

        for r in range(rows):
            move(x_hbm.at[r], (r + 1) * wide + 1, cols)
            move(left_hbm.at[r], (r + 1) * wide, 1)
            move(right_hbm.at[r], (r + 1) * wide + wide - 1, 1)
        move(low_hbm.at[0], 1, cols)
        move(high_hbm.at[0], (rows + 1) * wide + 1, cols)
        move(corner_low.at[0, pl.ds(0, 1)], 0, 1)
        move(corner_low.at[0, pl.ds(1, 1)], wide - 1, 1)
        move(corner_high.at[0, pl.ds(0, 1)], (rows + 1) * wide, 1)
        move(corner_high.at[0, pl.ds(1, 1)], (rows + 2) * wide - 1, 1)
        for c in copies:
            c.start()
        for c in copies:
            c.wait()
        if mode == "third":
            gram_ref[...] = jnp.zeros_like(gram_ref)
        if mode == "image":
            acc[...] = jnp.zeros_like(acc)

    lane = lax.broadcasted_iota(jnp.int32, (columns, basis), 1)
    made, held = [], []
    for j in range(cols):
        own = ext[(i + 1) * wide + j + 1]
        tiles = [ext[index_ref[i, j * neighbours + k]] for k in range(neighbours)]
        weights = near_ref[0, j]
        total = None
        for k in range(0, neighbours, 2):
            lhs = jnp.concatenate([tiles[k], tiles[k + 1]], axis=1)
            rhs = weights[k : k + 2].reshape(2 * basis, basis)
            part = jnp.dot(lhs, rhs, preferred_element_type=jnp.float32)
            total = part if total is None else total + part
        total = total + jnp.dot(own, self_ref[0, j], preferred_element_type=jnp.float32)
        live = lane < count_ref[i, j]
        total = jnp.where(live, total, 0.0)
        if mode != "image":
            value = (total - CENTER * own.astype(jnp.float32)) * INV_HALF
            if mode != "first":
                value = 2.0 * value - prev_ref[0, j].astype(jnp.float32)
            total = value
        result = total.astype(jnp.bfloat16)
        if mode != "image":
            out_ref[0, j] = result
        made.append(result)
        held.append(own)
    if mode == "third":
        wide_f = jnp.concatenate(made, axis=1)
        gram_ref[...] += nt_dot(wide_f, wide_f)
    if mode == "image":
        acc[...] += nt_dot(jnp.concatenate(held, axis=1), jnp.concatenate(made, axis=1))

        @pl.when(i == rows - 1)
        def _():
            share = columns // 4
            for s in range(4):
                first = pl.multiple_of(lax.rem(band_ref[0] + s, 4) * share, 8)
                pieces[s][0] = gram_in[pl.ds(first, share), :]
                pieces[s][1] = acc[pl.ds(first, share), :]


def apply_step(mode, x, halo, index, counts, band, h_self, h_near, prev=None, gram=None):
    rows, cols, columns, basis = x.shape
    neighbours = h_near.shape[2]
    dims = (rows, cols, columns, basis, neighbours)
    row = lambda i, *_: (i, 0, 0, 0)
    row5 = lambda i, *_: (i, 0, 0, 0, 0)
    fixed = lambda i, *_: (0, 0)
    in_specs = [ANY] * 7 + [
        pl.BlockSpec((1, cols, basis, basis), row),
        pl.BlockSpec((1, cols, neighbours, basis, basis), row5),
    ]
    args = [x, *halo, h_self, h_near]
    square = jax.ShapeDtypeStruct((columns, columns), jnp.float32)
    square_spec = pl.BlockSpec((columns, columns), fixed)
    scratch = [
        pltpu.VMEM(((rows + 2) * (cols + 2), columns, basis), jnp.bfloat16),
        pltpu.SemaphoreType.DMA,
    ]
    if prev is not None:
        in_specs.append(pl.BlockSpec((1, cols, columns, basis), row))
        args.append(prev)
    if mode == "image":
        in_specs.append(square_spec)
        args.append(gram)
        piece = (2, columns // 4, columns)
        out_shape = [jax.ShapeDtypeStruct(piece, jnp.float32)] * 4
        out_specs = [pl.BlockSpec(piece, lambda i, *_: (0, 0, 0))] * 4
        scratch.append(pltpu.VMEM((columns, columns), jnp.float32))
    else:
        out_shape = [jax.ShapeDtypeStruct(x.shape, jnp.bfloat16)]
        out_specs = [pl.BlockSpec((1, cols, columns, basis), row)]
        if mode == "third":
            out_shape.append(square)
            out_specs.append(square_spec)
    flops = 2 * rows * cols * columns * basis * basis * (neighbours + 1)
    return pl.pallas_call(
        functools.partial(step_kernel, mode, dims),
        out_shape=out_shape,
        grid_spec=pltpu.PrefetchScalarGridSpec(
            num_scalar_prefetch=3,
            grid=(rows,),
            in_specs=in_specs,
            out_specs=out_specs,
            scratch_shapes=scratch,
        ),
        compiler_params=pltpu.CompilerParams(
            dimension_semantics=("arbitrary",), vmem_limit_bytes=24 * 1024 * 1024
        ),
        cost_estimate=pl.CostEstimate(flops=flops, bytes_accessed=10_000_000, transcendentals=0),
        name="step_" + mode,
    )(index, counts, band, *args)


def shifted(value, axes, count, step):
    return lax.ppermute(value, axes, [(p, (p + step) % count) for p in range(count)])


def on_device(elem, band, sizes, basis_counts, neighbour_codes, x_block, h_self, h_near):
    rows, cols, columns, basis = x_block.shape
    neighbours = neighbour_codes.shape[2]
    wide = cols + 2
    n_elem, n_band = sizes
    row_iota = lax.broadcasted_iota(jnp.int32, (rows, cols, neighbours), 0)
    col_iota = lax.broadcasted_iota(jnp.int32, (rows, cols, neighbours), 1)
    index = (
        (row_iota + neighbour_codes // 3) * wide + col_iota + neighbour_codes % 3
    ).reshape(rows, cols * neighbours)
    band_at = lax.axis_index(band).astype(jnp.int32)
    live = lax.broadcasted_iota(jnp.int32, x_block.shape, 3) < basis_counts[:, :, None, None]
    start = jnp.where(live, x_block, jnp.zeros_like(x_block))

    def exchange(v):
        left = shifted(v[:, cols - 1 :], band, n_band, 1)
        right = shifted(v[:, :1], band, n_band, -1)
        low = shifted(v[rows - 1 :], elem, n_elem, 1)
        high = shifted(v[:1], elem, n_elem, -1)
        edge_low = jnp.concatenate([left[rows - 1 :], right[rows - 1 :]], axis=1)
        edge_high = jnp.concatenate([left[:1], right[:1]], axis=1)
        corner_low = shifted(edge_low, elem, n_elem, 1)
        corner_high = shifted(edge_high, elem, n_elem, -1)
        return low, high, left, right, corner_low, corner_high

    def apply(mode, v, **more):
        return apply_step(
            mode, v, exchange(v), index, basis_counts, band_at.reshape(1), h_self, h_near, **more
        )

    (first,) = apply("first", start)
    (second,) = apply("second", first, prev=start)
    filtered, gram = apply("third", second, prev=first)
    pieces = apply("image", filtered, gram=gram)
    total = pieces[0]
    for s in range(1, n_band):
        total = total + shifted(pieces[s], band, n_band, s)

    def fold(value, axis, maps):
        moved = [lax.ppermute(value, axis, pairs) for pairs in maps]
        return sum(moved, value)

    total = fold(total, "x", [[(p, (p + s) % 4) for p in range(4)] for s in (1, 2, 3)])
    total = fold(total, "yl", [[(p, 1 - p) for p in range(2)]])
    for pairs in ([(p, p ^ 1) for p in range(8)], [(p, p ^ 2) for p in range(8)], [(p, 7 - p) for p in range(8)]):
        total = fold(total, "z", [pairs])
    normalizer = jnp.float32(rows * cols * n_elem * n_band * basis / 3.0)
    total = total / normalizer
    return filtered, total[0], total[1]


def solution(mesh):
    split = Mesh(mesh.devices.reshape(8, 2, 4, 2, 2), ("z", "yl", "x", "yh", "core"))
    elem, band = ("z", "yl", "x"), ("yh", "core")
    in_specs = (P(elem, band),) + tuple(P(elem, band, *[None] * n) for n in (1, 2, 2, 3))
    out_specs = (P(elem, band, None, None), P(band, None), P(band, None))
    body = functools.partial(on_device, elem, band, (64, 4))
    return jax.shard_map(body, mesh=split, in_specs=in_specs, out_specs=out_specs, check_vma=False)
```

```python
import functools

import jax
import jax.numpy as jnp
from jax import lax
from jax.experimental import pallas as pl
from jax.experimental.pallas import tpu as pltpu
from jax.sharding import Mesh, PartitionSpec as P


CENTER = 0.25
INV_HALF = 1.0 / 1.5
VMEM = pl.BlockSpec(memory_space=pltpu.VMEM)
SMEM = pl.BlockSpec(memory_space=pltpu.SMEM)
BF16, F32 = jnp.bfloat16, jnp.float32


def nt_dot(a, b):
    return lax.dot_general(a, b, (((1,), (1,)), ((), ())), preferred_element_type=F32)


def call(body, out_shape, args, in_specs=None, scratch=(), flops=0):
    return pl.pallas_call(
        body,
        out_shape=out_shape,
        in_specs=in_specs or [VMEM] * len(args),
        out_specs=jax.tree.map(lambda _: VMEM, out_shape),
        scratch_shapes=scratch,
        compiler_params=pltpu.CompilerParams(vmem_limit_bytes=16 * 1024 * 1024),
        cost_estimate=pl.CostEstimate(flops=flops, bytes_accessed=8_000_000, transcendentals=0),
    )(*args)


def step_kernel(mode, dims, *refs):
    rows, cols, columns, basis, neighbours = dims
    wide = cols + 2
    refs = list(refs)
    index, count, v, low, high, left, right, corner_left, corner_right, selfs, near = refs[:11]
    del refs[:11]
    prev = refs.pop(0) if mode in ("second", "third") else None
    if mode == "image":
        band, gram = refs[:2]
        pieces, ext, acc = refs[2:6], refs[6], refs[7]
        acc[...] = jnp.zeros_like(acc)
    else:
        out, col_right, col_left, row_low, row_high, ext = refs
    lane = lax.broadcasted_iota(jnp.int32, (columns, basis), 1)
    last = (rows + 1) * wide
    for j in range(cols):
        ext[1 + j] = low[0, j]
        ext[last + 1 + j] = high[0, j]
    for t in range(2):
        ext[t * last] = corner_left[t, 0]
        ext[t * last + wide - 1] = corner_right[t, 0]

    def fill(r, carry):
        for j in range(cols):
            ext[(r + 1) * wide + 1 + j] = v[r, j]
        ext[(r + 1) * wide] = left[r, 0]
        ext[(r + 1) * wide + wide - 1] = right[r, 0]
        return carry

    lax.fori_loop(0, rows, fill, 0)

    def one_row(i, carry):
        made, held = [], []
        for j in range(cols):
            own = ext[(i + 1) * wide + j + 1]
            tiles = [ext[index[i, j * neighbours + k]] for k in range(neighbours)]
            total = jnp.dot(own, selfs[i, j], preferred_element_type=F32)
            for k in range(0, neighbours, 2):
                lhs = jnp.concatenate([tiles[k], tiles[k + 1]], axis=1)
                rhs = near[i, j, k : k + 2].reshape(2 * basis, basis)
                total = total + jnp.dot(lhs, rhs, preferred_element_type=F32)
            total = jnp.where(lane < count[i, j], total, 0.0)
            if mode != "image":
                total = (total - CENTER * own.astype(F32)) * INV_HALF
                if mode != "first":
                    total = 2.0 * total - prev[i, j].astype(F32)
            result = total.astype(BF16)
            if mode == "image":
                made.append(result)
                held.append(own)
                continue
            out[i, j] = result
            if j == 0:
                col_left[i, 0] = result
            if j == cols - 1:
                col_right[i, 0] = result
        if mode == "image":
            acc[...] += nt_dot(jnp.concatenate(held, axis=1), jnp.concatenate(made, axis=1))
        return carry

    lax.fori_loop(0, rows, one_row, 0)
    if mode != "image":
        for j in range(cols):
            row_low[0, j] = out[rows - 1, j]
            row_high[0, j] = out[0, j]
        return
    share = columns // 4
    for s in range(4):
        first = pl.multiple_of(lax.rem(band[0] + s, 4) * share, 8)
        pieces[s][0] = gram[pl.ds(first, share), :]
        pieces[s][1] = acc[pl.ds(first, share), :]


def start_kernel(x, count, out, col_right, col_left, row_low, row_high):
    rows, cols, columns, basis = x.shape
    lane = lax.broadcasted_iota(jnp.int32, (columns, basis), 1)

    def one(r, c):
        for j in range(cols):
            value = jnp.where(lane < count[r, j], x[r, j].astype(F32), 0.0).astype(BF16)
            out[r, j] = value
            if j == 0:
                col_left[r, 0] = value
            if j == cols - 1:
                col_right[r, 0] = value
        return c

    lax.fori_loop(0, rows, one, 0)
    for j in range(cols):
        row_low[0, j] = out[rows - 1, j]
        row_high[0, j] = out[0, j]


def relay_kernel(low, high, send_right, send_left):
    cols = low.shape[1]
    for t, halo in enumerate((low, high)):
        send_right[t, 0] = halo[0, cols - 1]
        send_left[t, 0] = halo[0, 0]


def gram_kernel(v, gram):
    rows, cols = v.shape[:2]
    gram[...] = jnp.zeros_like(gram)

    def one(r, c):
        wide_v = jnp.concatenate([v[r, j] for j in range(cols)], axis=1)
        gram[...] += nt_dot(wide_v, wide_v)
        return c

    lax.fori_loop(0, rows, one, 0)


def shifted(value, axes, count, step):
    return lax.ppermute(value, axes, [(p, (p + step) % count) for p in range(count)])


def on_device(elem, band, sizes, basis_counts, neighbour_codes, x_block, h_self, h_near):
    rows, cols, columns, basis = x_block.shape
    neighbours = neighbour_codes.shape[2]
    dims = (rows, cols, columns, basis, neighbours)
    wide = cols + 2
    n_elem, n_band = sizes
    row_iota = lax.broadcasted_iota(jnp.int32, (rows, cols, neighbours), 0)
    col_iota = lax.broadcasted_iota(jnp.int32, (rows, cols, neighbours), 1)
    index = (
        (row_iota + neighbour_codes // 3) * wide + col_iota + neighbour_codes % 3
    ).reshape(rows, cols * neighbours)
    band_at = lax.axis_index(band).astype(jnp.int32).reshape(1)
    shape = lambda *s: jax.ShapeDtypeStruct(s, BF16)
    block = [
        shape(rows, cols, columns, basis),
        shape(rows, 1, columns, basis),
        shape(rows, 1, columns, basis),
        shape(1, cols, columns, basis),
        shape(1, cols, columns, basis),
    ]
    square = jax.ShapeDtypeStruct((columns, columns), F32)
    per_element = 2 * columns * basis * basis * (neighbours + 1)

    current = call(start_kernel, block, [x_block, basis_counts], in_specs=[VMEM, SMEM])
    older, gram = None, None
    for mode in ("first", "second", "third", "image"):
        v, col_right, col_left, row_low, row_high = current
        left = shifted(col_right, band, n_band, 1)
        right = shifted(col_left, band, n_band, -1)
        low = shifted(row_low, elem, n_elem, 1)
        high = shifted(row_high, elem, n_elem, -1)
        relay = [shape(2, 1, columns, basis)] * 2
        send_right, send_left = call(relay_kernel, relay, [low, high])
        corner_left = shifted(send_right, band, n_band, 1)
        corner_right = shifted(send_left, band, n_band, -1)
        prev = [older] if mode in ("second", "third") else []
        args = [index, basis_counts, v, low, high, left, right, corner_left, corner_right]
        args += [h_self, h_near, *prev]
        specs = [SMEM, SMEM] + [VMEM] * (len(args) - 2)
        scratch = [pltpu.VMEM(((rows + 2) * wide, columns, basis), BF16)]
        if mode == "image":
            gram = call(gram_kernel, square, [v], flops=2 * 32 * columns * columns * basis)
            args += [band_at, gram]
            specs += [SMEM, VMEM]
            scratch.append(pltpu.VMEM((columns, columns), F32))
            out_shape = [jax.ShapeDtypeStruct((2, columns // 4, columns), F32)] * 4
        else:
            out_shape = block
        done = call(
            functools.partial(step_kernel, mode, dims),
            out_shape,
            args,
            in_specs=specs,
            scratch=scratch,
            flops=32 * per_element,
        )
        if mode == "image":
            filtered, pieces = v, done
        else:
            older, current = v, done

    total = pieces[0]
    for s in range(1, n_band):
        total = total + shifted(pieces[s], band, n_band, s)

    def fold(value, axis, maps):
        moved = [lax.ppermute(value, axis, pairs) for pairs in maps]
        return sum(moved, value)

    total = fold(total, "x", [[(p, (p + s) % 4) for p in range(4)] for s in (1, 2, 3)])
    total = fold(total, "yl", [[(p, 1 - p) for p in range(2)]])
    for pairs in ([(p, p ^ 1) for p in range(8)], [(p, p ^ 2) for p in range(8)], [(p, 7 - p) for p in range(8)]):
        total = fold(total, "z", [pairs])
    normalizer = jnp.float32(rows * cols * n_elem * n_band * basis / 3.0)
    total = total / normalizer
    return filtered, total[0], total[1]


def solution(mesh):
    split = Mesh(mesh.devices.reshape(8, 2, 4, 2, 2), ("z", "yl", "x", "yh", "core"))
    elem, band = ("z", "yl", "x"), ("yh", "core")
    in_specs = (P(elem, band),) + tuple(P(elem, band, *[None] * n) for n in (1, 2, 2, 3))
    out_specs = (P(elem, band, None, None), P(band, None), P(band, None))
    body = functools.partial(on_device, elem, band, (64, 4))
    return jax.shard_map(body, mesh=split, in_specs=in_specs, out_specs=out_specs, check_vma=False)
```

```python
import functools

import jax
import jax.numpy as jnp
from jax import lax
from jax.experimental import pallas as pl
from jax.experimental.pallas import tpu as pltpu
from jax.sharding import Mesh, PartitionSpec as P


CENTER = 0.25
INV_HALF = 1.0 / 1.5
VMEM = pl.BlockSpec(memory_space=pltpu.VMEM)
HBM = pl.BlockSpec(memory_space=pltpu.HBM)
SMEM = pl.BlockSpec(memory_space=pltpu.SMEM)
BF16, F32 = jnp.bfloat16, jnp.float32


def nt_dot(a, b):
    return lax.dot_general(a, b, (((1,), (1,)), ((), ())), preferred_element_type=F32)


def call(body, out_shape, args, in_specs=None, out_specs=None, scratch=(), flops=0):
    return pl.pallas_call(
        body,
        out_shape=out_shape,
        in_specs=in_specs or [VMEM] * len(args),
        out_specs=out_specs or jax.tree.map(lambda _: VMEM, out_shape),
        scratch_shapes=scratch,
        compiler_params=pltpu.CompilerParams(vmem_limit_bytes=16 * 1024 * 1024),
        cost_estimate=pl.CostEstimate(flops=flops, bytes_accessed=8_000_000, transcendentals=0),
    )(*args)


def step_kernel(mode, dims, *refs):
    rows, cols, columns, basis, neighbours = dims
    wide = cols + 2
    refs = list(refs)
    index, count, v, low, high, left, right, corner_left, corner_right, selfs, near = refs[:11]
    del refs[:11]
    prev = refs.pop(0) if mode in ("second", "third") else None
    if mode == "image":
        band, gram = refs[:2]
        pieces = refs[2:6]
        ext, acc, held_self, held_near, sems = refs[6:11]
        self_hbm, near_hbm, selfs, near = selfs, near, held_self, held_near
        for r in range(rows):
            pltpu.make_async_copy(self_hbm.at[r], selfs.at[r], sems.at[0, r]).start()
            pltpu.make_async_copy(near_hbm.at[r], near.at[r], sems.at[1, r]).start()
    else:
        out, col_right, col_left, row_low, row_high = refs[:5]
        ext = refs[5]
    if mode == "image":
        acc[...] = jnp.zeros_like(acc)
    lane = lax.broadcasted_iota(jnp.int32, (columns, basis), 1)
    last = (rows + 1) * wide
    for j in range(cols):
        ext[1 + j] = low[0, j]
        ext[last + 1 + j] = high[0, j]
    for t in range(2):
        ext[t * last] = corner_left[t, 0]
        ext[t * last + wide - 1] = corner_right[t, 0]

    def fill(r, carry):
        for j in range(cols):
            ext[(r + 1) * wide + 1 + j] = v[r, j]
        ext[(r + 1) * wide] = left[r, 0]
        ext[(r + 1) * wide + wide - 1] = right[r, 0]
        return carry

    lax.fori_loop(0, rows, fill, 0)

    def one_row(i, carry):
        made, held = [], []
        if mode == "image":
            pltpu.make_async_copy(self_hbm.at[i], selfs.at[i], sems.at[0, i]).wait()
            pltpu.make_async_copy(near_hbm.at[i], near.at[i], sems.at[1, i]).wait()
        for j in range(cols):
            own = ext[(i + 1) * wide + j + 1]
            tiles = [ext[index[i, j * neighbours + k]] for k in range(neighbours)]
            total = jnp.dot(own, selfs[i, j], preferred_element_type=F32)
            for k in range(0, neighbours, 2):
                lhs = jnp.concatenate([tiles[k], tiles[k + 1]], axis=1)
                rhs = near[i, j, k : k + 2].reshape(2 * basis, basis)
                total = total + jnp.dot(lhs, rhs, preferred_element_type=F32)
            total = jnp.where(lane < count[i, j], total, 0.0)
            if mode != "image":
                total = (total - CENTER * own.astype(F32)) * INV_HALF
                if mode != "first":
                    total = 2.0 * total - prev[i, j].astype(F32)
            result = total.astype(BF16)
            if mode == "image":
                made.append(result)
                held.append(own)
                continue
            out[i, j] = result
            if j == 0:
                col_left[i, 0] = result
            if j == cols - 1:
                col_right[i, 0] = result
        if mode == "image":
            acc[...] += nt_dot(jnp.concatenate(held, axis=1), jnp.concatenate(made, axis=1))
        return carry

    lax.fori_loop(0, rows, one_row, 0)
    if mode != "image":
        for j in range(cols):
            row_low[0, j] = out[rows - 1, j]
            row_high[0, j] = out[0, j]
        return
    share = columns // 4
    for s in range(4):
        first = pl.multiple_of(lax.rem(band[0] + s, 4) * share, 8)
        pieces[s][0] = gram[pl.ds(first, share), :]
        pieces[s][1] = acc[pl.ds(first, share), :]


def start_kernel(x_hbm, count, out, col_right, col_left, row_low, row_high, x, sems):
    rows, cols, columns, basis = x.shape
    for r in range(rows):
        pltpu.make_async_copy(x_hbm.at[r], x.at[r], sems.at[r]).start()
    lane = lax.broadcasted_iota(jnp.int32, (columns, basis), 1)

    def one(r, c):
        pltpu.make_async_copy(x_hbm.at[r], x.at[r], sems.at[r]).wait()
        for j in range(cols):
            value = jnp.where(lane < count[r, j], x[r, j].astype(F32), 0.0).astype(BF16)
            out[r, j] = value
            if j == 0:
                col_left[r, 0] = value
            if j == cols - 1:
                col_right[r, 0] = value
        return c

    lax.fori_loop(0, rows, one, 0)
    for j in range(cols):
        row_low[0, j] = out[rows - 1, j]
        row_high[0, j] = out[0, j]


def load_kernel(self_hbm, near_hbm, selfs, near, sems):
    copies = []
    for r in range(selfs.shape[0]):
        copies.append(pltpu.make_async_copy(self_hbm.at[r], selfs.at[r], sems.at[0, r]))
        copies.append(pltpu.make_async_copy(near_hbm.at[r], near.at[r], sems.at[1, r]))
    for c in copies:
        c.start()
    for c in copies:
        c.wait()


def relay_kernel(low, high, send_right, send_left):
    cols = low.shape[1]
    for t, halo in enumerate((low, high)):
        send_right[t, 0] = halo[0, cols - 1]
        send_left[t, 0] = halo[0, 0]


def gram_kernel(v, gram, whole, sems):
    rows, cols = v.shape[:2]
    copies = [pltpu.make_async_copy(v.at[r], whole.at[r], sems.at[r]) for r in range(rows)]
    for c in copies:
        c.start()
    gram[...] = jnp.zeros_like(gram)

    def one(r, carry):
        wide_v = jnp.concatenate([v[r, j] for j in range(cols)], axis=1)
        gram[...] += nt_dot(wide_v, wide_v)
        return carry

    lax.fori_loop(0, rows, one, 0)
    for c in copies:
        c.wait()


def shifted(value, axes, count, step):
    return lax.ppermute(value, axes, [(p, (p + step) % count) for p in range(count)])


def on_device(elem, band, sizes, basis_counts, neighbour_codes, x_block, h_self, h_near):
    rows, cols, columns, basis = x_block.shape
    neighbours = neighbour_codes.shape[2]
    dims = (rows, cols, columns, basis, neighbours)
    wide = cols + 2
    n_elem, n_band = sizes
    row_iota = lax.broadcasted_iota(jnp.int32, (rows, cols, neighbours), 0)
    col_iota = lax.broadcasted_iota(jnp.int32, (rows, cols, neighbours), 1)
    index = (
        (row_iota + neighbour_codes // 3) * wide + col_iota + neighbour_codes % 3
    ).reshape(rows, cols * neighbours)
    band_at = lax.axis_index(band).astype(jnp.int32).reshape(1)
    shape = lambda *s: jax.ShapeDtypeStruct(s, BF16)
    block = [
        shape(rows, cols, columns, basis),
        shape(rows, 1, columns, basis),
        shape(rows, 1, columns, basis),
        shape(1, cols, columns, basis),
        shape(1, cols, columns, basis),
    ]
    square = jax.ShapeDtypeStruct((columns, columns), F32)
    per_element = 2 * columns * basis * basis * (neighbours + 1)

    x_hbm, self_hbm, near_hbm = (
        pltpu.with_memory_space_constraint(a, pltpu.HBM) for a in (x_block, h_self, h_near)
    )
    current = call(
        start_kernel,
        block,
        [x_hbm, basis_counts],
        in_specs=[HBM, SMEM],
        scratch=[pltpu.VMEM(x_block.shape, BF16), pltpu.SemaphoreType.DMA((rows,))],
    )
    older = None
    for step, mode in enumerate(("first", "second", "third", "image")):
        v, col_right, col_left, row_low, row_high = current
        left = shifted(col_right, band, n_band, 1)
        right = shifted(col_left, band, n_band, -1)
        low = shifted(row_low, elem, n_elem, 1)
        high = shifted(row_high, elem, n_elem, -1)
        relay = [shape(2, 1, columns, basis)] * 2
        send_right, send_left = call(relay_kernel, relay, [low, high])
        corner_left = shifted(send_right, band, n_band, 1)
        corner_right = shifted(send_left, band, n_band, -1)
        if step == 0:
            resident = call(
                load_kernel,
                [jax.ShapeDtypeStruct(a.shape, BF16) for a in (h_self, h_near)],
                [self_hbm, near_hbm],
                in_specs=[HBM, HBM],
                scratch=[pltpu.SemaphoreType.DMA((2, rows))],
            )
        prev = [older] if mode in ("second", "third") else []
        args = [index, basis_counts, v, low, high, left, right, corner_left, corner_right]
        args += [self_hbm, near_hbm] if mode == "image" else [*resident, *prev]
        specs = [SMEM, SMEM] + [VMEM] * 7 + [HBM if mode == "image" else VMEM] * 2
        specs += [VMEM] * len(prev)
        scratch = [
            pltpu.VMEM(((rows + 2) * wide, columns, basis), BF16),
        ]
        if mode == "image":
            gram, filtered = call(
                gram_kernel,
                [square, block[0]],
                [v],
                out_specs=[VMEM, HBM],
                scratch=[pltpu.SemaphoreType.DMA((rows,))],
                flops=2 * rows * cols * columns * columns * basis,
            )
            args += [band_at, gram]
            specs += [SMEM, VMEM]
            scratch += [
                pltpu.VMEM((columns, columns), F32),
                pltpu.VMEM(h_self.shape, BF16),
                pltpu.VMEM(h_near.shape, BF16),
                pltpu.SemaphoreType.DMA((2, rows)),
            ]
            out_shape = [jax.ShapeDtypeStruct((2, columns // 4, columns), F32)] * 4
        else:
            out_shape = block
        done = call(
            functools.partial(step_kernel, mode, dims),
            out_shape,
            args,
            in_specs=specs,
            scratch=scratch,
            flops=32 * per_element,
        )
        if mode == "image":
            pieces = done
        else:
            older, current = v, done[:5]

    total = pieces[0]
    for s in range(1, n_band):
        total = total + shifted(pieces[s], band, n_band, s)

    def fold(value, axis, maps):
        moved = [lax.ppermute(value, axis, pairs) for pairs in maps]
        return sum(moved, value)

    total = fold(total, "x", [[(p, (p + s) % 4) for p in range(4)] for s in (1, 2, 3)])
    total = fold(total, "yl", [[(p, 1 - p) for p in range(2)]])
    total = fold(total, "z", [[(p, p ^ 1) for p in range(8)]])
    total = fold(total, "z", [[(p, p ^ 2) for p in range(8)]])
    total = fold(total, "z", [[(p, 7 - p) for p in range(8)]])
    normalizer = jnp.float32(rows * cols * n_elem * n_band * basis / 3.0)
    total = total / normalizer
    return filtered, total[0], total[1]


def solution(mesh):
    split = Mesh(mesh.devices.reshape(8, 2, 4, 2, 2), ("z", "yl", "x", "yh", "core"))
    elem, band = ("z", "yl", "x"), ("yh", "core")
    in_specs = (P(elem, band),) + tuple(P(elem, band, *[None] * n) for n in (1, 2, 2, 3))
    out_specs = (P(elem, band, None, None), P(band, None), P(band, None))
    body = functools.partial(on_device, elem, band, (64, 4))
    return jax.shard_map(body, mesh=split, in_specs=in_specs, out_specs=out_specs, check_vma=False)
```
